32 devices in a mesh: row: 8 (over y, x, core), col: 4 (over z).
Axes of the slice: x: 2, y: 2, z: 4, core: 2. Of those that a mesh axis runs over, the one named last changes fastest.
Arguments:
- rhs: float32 [32, 1024, 4096], P(None, 'row', 'col'), may hold values from -6 to 6
- factor: bfloat16 [32, 1024, 4, 1024], P(None, 'row', None, 'col'), may hold values from -0.09375 to 0.09375
- diag_inverse: bfloat16 [4, 1024, 1024], P(None, 'row'), may hold values from -1.5 to 1.5, as said below
Outputs:
- solution: float32 [4, 1024, 4096], P(None, 'row', 'col')
- remaining: float32 [28, 1024, 4096], P(None, 'row', 'col')
The draws below stay inside these ranges and needn't reach their ends.
Inputs may be any that keep to these rules, and one draw needn't show every extreme that they name: Each diag_inverse[k] is lower triangular with diagonal entries from 0.5 to 1.5.
All inputs are finite; a program needn't handle non-finite values.
Results may differ from the reference program's by a relative error of at most 0.0044.
Values may be sent and summed in bfloat16 or wider, within the bound.
A program may use at most 192 MiB of HBM per device.

```python
import jax
import jax.numpy as jnp
from jax import lax

BLOCK = 1024
STEPS = 4
BLOCKS = 32
RHS = 4096


def draw_diag_inverse(key, part):
    key_below = jax.random.fold_in(key, 11)
    key_diagonal = jax.random.fold_in(key, 23)
    shape = (STEPS, BLOCK, BLOCK)
    row_index = lax.broadcasted_iota(jnp.int32, shape, 1)
    col_index = lax.broadcasted_iota(jnp.int32, shape, 2)
    below = jnp.clip(jax.random.normal(key_below, shape, jnp.float32), -6.0, 6.0) * BLOCK ** (-0.5)
    diagonal_values = jax.random.uniform(key_diagonal, shape, jnp.float32, 0.5, 1.5)
    return jnp.where(row_index > col_index, below, jnp.where(row_index == col_index, diagonal_values, 0.0)).astype(jnp.bfloat16)


def block_levels(stream_key, shape, pieces, low, largest):
    def one(axis_at, shards_of):
        heights = jax.random.uniform(jax.random.fold_in(jax.random.fold_in(stream_key, 6), axis_at), (shards_of,), jnp.float32, low / len(pieces), largest / len(pieces))
        return jnp.repeat(jnp.exp(heights), shape[axis_at] // shards_of).reshape((-1,) + (1,) * (len(shape) - axis_at - 1))

    gain = one(*pieces[0])
    for cut in pieces[1:]:
        gain = gain * one(*cut)
    return gain


def normal_values(stream_key, shape, spread, most, shards=(), dtype=jnp.bfloat16):
    gain = block_levels(stream_key, shape, shards, -0.22, 0.18) if shards else 1.0
    array = jax.random.normal(stream_key, shape, jnp.float32) * spread * gain
    return jnp.minimum(jnp.maximum(array, -most), most).astype(dtype)


def setup_inputs(seed: int = 0) -> dict:
    key_of = jax.random.split(jax.random.key(seed), 4)
    return {
        "rhs": normal_values(key_of[0], (BLOCKS, BLOCK, RHS), 1.0, 6.0, ((1, 8), (2, 4)), jnp.float32),
        "factor": normal_values(key_of[1], (BLOCKS, BLOCK, STEPS, BLOCK), (STEPS * BLOCK) ** -0.5, 0.09375, ((1, 8), (3, 4))),
        "diag_inverse": draw_diag_inverse(jax.random.fold_in(key_of[3], 71), 0),
    }


def reference(rhs, factor, diag_inverse):
    pending = [rhs[index] for index in range(BLOCKS)]
    solved_list = []
    for section in range(STEPS):
        current = pending[section].astype(jnp.bfloat16)
        result = jnp.dot(diag_inverse[section], current, preferred_element_type=jnp.float32)
        solved_list.append(result)
        solved_rows = result.astype(jnp.bfloat16)
        for index in range(section + 1, BLOCKS):
            update = jnp.dot(factor[index, :, section, :], solved_rows, preferred_element_type=jnp.float32)
            pending[index] = pending[index] - update
    remaining = jnp.stack(pending[STEPS:])
    return jnp.stack(solved_list), remaining
```

```python
import jax
import jax.numpy as jnp
from jax import lax
from jax.sharding import PartitionSpec as P

STEPS = 4
GATHERED = (7, 7, 7, 7)
REDUCED = ()


def dot(a, b):
    return jnp.dot(a, b, preferred_element_type=jnp.float32)


def up(n, distance):
    return [(z, z + 1) for z in range(distance - 1, n - 1)]


def down(n, distance):
    return [(z, z - 1) for z in range(1, n - distance + 1)]


class Line:
    def __init__(self, own, n):
        self.n = n
        self.own = own
        self.below = [own]
        self.above = [own]

    def hop(self):
        distance = len(self.below)
        self.below.append(lax.ppermute(self.below[-1], "col", up(self.n, distance)))
        self.above.append(lax.ppermute(self.above[-1], "col", down(self.n, distance)))

    def tie(self, value):
        value, self.below[-1], self.above[-1] = lax.optimization_barrier((value, self.below[-1], self.above[-1]))
        return value

    def parts(self):
        while len(self.below) < self.n:
            self.hop()
        z = lax.axis_index("col")
        return [self.own] + [
            jnp.where(z + d < self.n, self.above[d], self.below[self.n - d]) for d in range(1, self.n)
        ]


def reduce_line(products, n):
    upward = downward = None
    for distance in range(n - 1, 0, -1):
        u = products[distance]
        v = products[n - distance]
        if upward is not None:
            u = u + upward.astype(jnp.float32)
            v = v + downward.astype(jnp.float32)
        upward = lax.ppermute(u.astype(jnp.bfloat16), "col", [(z, z + 1) for z in range(n - distance)])
        downward = lax.ppermute(v.astype(jnp.bfloat16), "col", [(z, z - 1) for z in range(distance, n)])
    return products[0] + upward.astype(jnp.float32) + downward.astype(jnp.float32)


def shards(rhs, factor, diag_inverse):
    block_count, tile_rows, width = rhs.shape
    panel = factor.shape[3]
    n = lax.axis_size("col")
    rows_n = lax.axis_size("row")
    z = lax.axis_index("col")
    r = lax.axis_index("row")

    first = rhs[0].astype(jnp.bfloat16)
    whole = lax.all_gather(first, "row", axis=0, tiled=True)
    head = factor[1:STEPS, :, : STEPS - 1, :].reshape((STEPS - 1) * tile_rows, (STEPS - 1) * panel)
    head_parts = jnp.stack(Line(head, n).parts())
    head_parts = head_parts.reshape(n, STEPS - 1, tile_rows, STEPS - 1, panel)

    tiles = []
    start = STEPS
    for count in GATHERED:
        flat = factor[start : start + count].reshape(count * tile_rows, STEPS * panel)
        tiles.append((start, count, Line(flat, n)))
        start += count

    order = [line for _ in range(1, n) for _, _, line in tiles]

    def advance(value):
        if not order:
            return value
        line = order.pop(0)
        line.hop()
        return line.tie(value)

    solved = []
    solution_list = []
    for k in range(STEPS):
        if k:
            total = rhs[k]
            for d in range(n):
                part = lax.dynamic_slice_in_dim(jnp.stack(solved), ((z + d) % n) * panel, panel, axis=1)
                total = total - dot(head_parts[d, k - 1, :, :k, :].reshape(tile_rows, k * panel), part.reshape(k * panel, width))
            whole = lax.all_gather(total.astype(jnp.bfloat16), "row", axis=0, tiled=True)
        own = dot(diag_inverse[k], advance(whole))
        solution_list.append(own)
        solved.append(advance(lax.all_gather(own.astype(jnp.bfloat16), "row", axis=0, tiled=True)))
    stacked = jnp.stack(solved)

    def panel_of(d):
        return lax.dynamic_slice_in_dim(stacked, ((z + d) % n) * panel, panel, axis=1).reshape(STEPS * panel, width)

    panels = [panel_of(d) for d in range(n)]
    outs = []
    for begin, count, line in tiles:
        parts = line.parts()
        total = rhs[begin : begin + count].reshape(count * tile_rows, width)
        for d in range(n):
            total = total - dot(parts[d], panels[d])
        outs.append(total.reshape(count, tile_rows, width))

    if REDUCED:
        share = panel // rows_n
        pieces = []
        for d in range(1, n):
            target = (z - d) % n
            piece = lax.dynamic_slice_in_dim(stacked, target * panel + r * share, share, axis=1)
            pieces.append(lax.ppermute(piece, "col", [(s, (s - d) % n) for s in range(n)]))
        spread = lax.all_gather(jnp.concatenate(pieces, axis=2), "row", axis=1, tiled=True)
        spread = spread.reshape(STEPS * panel, (n - 1) * width)
        own_panels = [panels[0]] + [spread[:, d * width : (d + 1) * width] for d in range(n - 1)]
        for count in REDUCED:
            flat = factor[start : start + count].reshape(count * tile_rows, STEPS * panel)
            total = reduce_line([dot(flat, p) for p in own_panels], n)
            outs.append(rhs[start : start + count] - total.reshape(count, tile_rows, width))
            start += count
    return jnp.stack(solution_list), jnp.concatenate(outs)


def solution(mesh):
    in_specs = (P(None, "row", "col"), P(None, "row", None, "col"), P(None, "row", None))
    out_specs = (P(None, "row", "col"), P(None, "row", "col"))
    return jax.shard_map(shards, mesh=mesh, in_specs=in_specs, out_specs=out_specs, check_vma=False)
```

```python
import functools

import jax
import jax.numpy as jnp
from jax import lax
from jax.experimental import pallas as pl
from jax.experimental.pallas import tpu as pltpu
from jax.sharding import PartitionSpec as P

STEPS = 4
GATHERED = (9, 9)
REDUCED = (5, 5)


def dot(a, b):
    return jnp.dot(a, b, preferred_element_type=jnp.float32)


def up(n, distance):
    return [(z, z + 1) for z in range(distance - 1, n - 1)]


def down(n, distance):
    return [(z, z - 1) for z in range(1, n - distance + 1)]


class Line:
    def __init__(self, own, n):
        self.n = n
        self.own = own
        self.below = [own]
        self.above = [own]

    def hop(self):
        distance = len(self.below)
        self.below.append(lax.ppermute(self.below[-1], "col", up(self.n, distance)))
        self.above.append(lax.ppermute(self.above[-1], "col", down(self.n, distance)))

    def tie(self, value):
        value, self.below[-1], self.above[-1] = lax.optimization_barrier((value, self.below[-1], self.above[-1]))
        return value

    def parts(self):
        while len(self.below) < self.n:
            self.hop()
        z = lax.axis_index("col")
        return [self.own] + [
            jnp.where(z + d < self.n, self.above[d], self.below[self.n - d]) for d in range(1, self.n)
        ]


class Sums:
    def __init__(self, products, n):
        self.n = n
        self.products = products
        self.distance = n
        self.upward = self.downward = None

    def hop(self):
        self.distance -= 1
        u = self.products[self.distance]
        v = self.products[self.n - self.distance]
        if self.upward is not None:
            u = u + self.upward.astype(jnp.float32)
            v = v + self.downward.astype(jnp.float32)
        self.upward = lax.ppermute(u.astype(jnp.bfloat16), "col", [(z, z + 1) for z in range(self.n - self.distance)])
        self.downward = lax.ppermute(v.astype(jnp.bfloat16), "col", [(z, z - 1) for z in range(self.distance, self.n)])

    def total(self):
        return self.products[0] + self.upward.astype(jnp.float32) + self.downward.astype(jnp.float32)


def substitute_kernel(rows_n, rhs_ref, head_ref, inverse_ref, solution_ref, solved_ref, current, solved, send_sem, recv_sem, out_sem):
    r = lax.axis_index("row")
    pair = r + 1 - 2 * (r % 2)
    half = rows_n // 2
    tile_rows, width = rhs_ref.shape[1:]
    columns = 256
    own_rows = pl.ds(pl.multiple_of(r * tile_rows, tile_rows), tile_rows)

    barrier = pltpu.get_barrier_semaphore()
    for j in range(1, rows_n):
        pl.semaphore_signal(barrier, inc=1, device_id={"row": (r + j) % rows_n}, device_id_type=pl.DeviceIdType.MESH)
    pl.semaphore_wait(barrier, rows_n - 1)

    sent = []

    def copy(buffer, exchange, owner, slot, device):
        rows = buffer.at[pl.ds(pl.multiple_of(owner * tile_rows, tile_rows), tile_rows)]
        return pltpu.make_async_remote_copy(
            src_ref=rows,
            dst_ref=rows,
            send_sem=send_sem.at[exchange, slot],
            recv_sem=recv_sem.at[exchange, owner],
            device_id={"row": device},
            device_id_type=pl.DeviceIdType.MESH,
        )

    def gather(buffer, exchange):
        for j in range(half - 1, 0, -1):
            sent.append(copy(buffer, exchange, r, j, (r + 2 * j) % rows_n))
            sent[-1].start()
        sent.append(copy(buffer, exchange, r, 0, pair))
        sent[-1].start()
        for j in range(1, half):
            owner = (r + rows_n - 2 * j) % rows_n
            onward = copy(buffer, exchange, owner, half + j, pair)
            onward.wait_recv()
            onward.start()
            sent.append(onward)
        for j in range(half):
            copy(buffer, exchange, (pair + rows_n - 2 * j) % rows_n, 0, pair).wait_recv()

    outward = []
    for k in range(rhs_ref.shape[0]):

        @pl.loop(0, width // columns)
        def _(c):
            cols = pl.ds(pl.multiple_of(c * columns, columns), columns)
            total = rhs_ref[k, :, cols]
            for j in range(k):
                total = total - dot(head_ref[k - 1, j], solved[j, :, cols])
            current[k, own_rows, cols] = total.astype(jnp.bfloat16)

        gather(current.at[k], 2 * k)

        @pl.loop(0, width // columns)
        def _(c):
            cols = pl.ds(pl.multiple_of(c * columns, columns), columns)
            own = dot(inverse_ref[k], current[k, :, cols])
            solution_ref[k, :, cols] = own
            solved[k, own_rows, cols] = own.astype(jnp.bfloat16)

        gather(solved.at[k], 2 * k + 1)
        outward.append(pltpu.make_async_copy(solved.at[k], solved_ref.at[k], out_sem.at[k]))
        outward[-1].start()
    for item in sent:
        item.wait_send()
    for item in outward:
        item.wait()


def substitute(rhs, head, inverse, rows_n):
    steps, tile_rows, width = rhs.shape
    block = rows_n * tile_rows
    vmem = pl.BlockSpec(memory_space=pltpu.VMEM)
    return pl.pallas_call(
        functools.partial(substitute_kernel, rows_n),
        out_shape=(
            jax.ShapeDtypeStruct((steps, tile_rows, width), jnp.float32),
            jax.ShapeDtypeStruct((steps, block, width), jnp.bfloat16),
        ),
        in_specs=[vmem] * 3,
        out_specs=(vmem, pl.BlockSpec(memory_space=pl.ANY)),
        scratch_shapes=[
            pltpu.VMEM((steps, block, width), jnp.bfloat16),
            pltpu.VMEM((steps, block, width), jnp.bfloat16),
            pltpu.SemaphoreType.DMA((2 * steps, rows_n)),
            pltpu.SemaphoreType.DMA((2 * steps, rows_n)),
            pltpu.SemaphoreType.DMA((steps,)),
        ],
        compiler_params=pltpu.CompilerParams(collective_id=0, has_side_effects=True, vmem_limit_bytes=40 * 2**20),
        cost_estimate=pl.CostEstimate(flops=12 * 10**13, bytes_accessed=2**24, transcendentals=0),
    )(rhs, head, inverse)


def shards(rhs, factor, diag_inverse):
    block_count, tile_rows, width = rhs.shape
    panel = factor.shape[3]
    n = lax.axis_size("col")
    rows_n = lax.axis_size("row")
    z = lax.axis_index("col")
    r = lax.axis_index("row")

    head = factor[1:STEPS, :, : STEPS - 1, :].transpose(0, 2, 1, 3)
    head = lax.all_gather(head, "col", axis=3, tiled=True)

    tiles = []
    start = STEPS
    for count in GATHERED:
        flat = factor[start : start + count].reshape(count * tile_rows, STEPS * panel)
        head, flat = lax.optimization_barrier((head, flat))
        tiles.append((start, count, Line(flat, n)))
        start += count

    solution_rows, stacked = substitute(rhs[:STEPS], head, diag_inverse, rows_n)
    for _, _, line in tiles:
        line.hop()
        stacked = line.tie(stacked)

    def panel_of(d):
        return lax.dynamic_slice_in_dim(stacked, ((z + d) % n) * panel, panel, axis=1).reshape(STEPS * panel, width)

    panels = [panel_of(d) for d in range(n)]
    share = panel // rows_n
    pieces = []
    for d in range(1, n):
        target = (z - d) % n
        piece = lax.dynamic_slice_in_dim(stacked, target * panel + r * share, share, axis=1)
        pieces.append(lax.ppermute(piece, "col", [(s, (s - d) % n) for s in range(n)]))
    spread = lax.all_gather(jnp.concatenate(pieces, axis=2), "row", axis=1, tiled=True)
    spread = spread.reshape(STEPS * panel, (n - 1) * width)
    own_panels = [panels[0]] + [spread[:, d * width : (d + 1) * width] for d in range(n - 1)]
    sums = []
    for count in REDUCED:
        flat = factor[start : start + count].reshape(count * tile_rows, STEPS * panel)
        sums.append((start, count, Sums([dot(flat, p) for p in own_panels], n)))
        start += count

    for step in range(1, n):
        if step < n - 1:
            for _, _, line in tiles:
                line.hop()
        for _, _, item in sums:
            item.hop()
        moved = [(line.below[-1], line.above[-1]) for _, _, line in tiles]
        carried = [(item.upward, item.downward) for _, _, item in sums]
        if step < n - 1:
            moved, carried = lax.optimization_barrier((moved, carried))
        for (_, _, line), (below, above) in zip(tiles, moved):
            line.below[-1], line.above[-1] = below, above
        for (_, _, item), (upward, downward) in zip(sums, carried):
            item.upward, item.downward = upward, downward

    outs = []
    for begin, count, line in tiles:
        parts = line.parts()
        total = rhs[begin : begin + count].reshape(count * tile_rows, width)
        for d in range(n):
            total = total - dot(parts[d], panels[d])
        outs.append(total.reshape(count, tile_rows, width))
    for begin, count, item in sums:
        outs.append(rhs[begin : begin + count] - item.total().reshape(count, tile_rows, width))
    return solution_rows, jnp.concatenate(outs)


def solution(mesh):
    in_specs = (P(None, "row", "col"), P(None, "row", None, "col"), P(None, "row", None))
    out_specs = (P(None, "row", "col"), P(None, "row", "col"))
    return jax.shard_map(shards, mesh=mesh, in_specs=in_specs, out_specs=out_specs, check_vma=False)
```

```python
import functools

import jax
import jax.numpy as jnp
from jax import lax
from jax.experimental import pallas as pl
from jax.experimental.pallas import tpu as pltpu
from jax.sharding import PartitionSpec as P

STEPS = 4
GATHERED = (20,)
REDUCED = (8,)


def dot(a, b):
    return jnp.dot(a, b, preferred_element_type=jnp.float32)


def up(n, distance):
    return [(z, z + 1) for z in range(distance - 1, n - 1)]


def down(n, distance):
    return [(z, z - 1) for z in range(1, n - distance + 1)]


class Line:
    def __init__(self, own, n):
        self.n = n
        self.own = own
        self.below = [own]
        self.above = [own]

    def hop(self):
        distance = len(self.below)
        self.below.append(lax.ppermute(self.below[-1], "col", up(self.n, distance)))
        self.above.append(lax.ppermute(self.above[-1], "col", down(self.n, distance)))

    def tie(self, value):
        value, self.below[-1], self.above[-1] = lax.optimization_barrier((value, self.below[-1], self.above[-1]))
        return value

    def parts(self):
        while len(self.below) < self.n:
            self.hop()
        z = lax.axis_index("col")
        return [self.own] + [
            jnp.where(z + d < self.n, self.above[d], self.below[self.n - d]) for d in range(1, self.n)
        ]


class Sums:
    def __init__(self, products, n):
        self.n = n
        self.products = products
        self.distance = n
        self.upward = self.downward = None

    def hop(self):
        self.distance -= 1
        u = self.products[self.distance]
        v = self.products[self.n - self.distance]
        if self.upward is not None:
            u = u + self.upward.astype(jnp.float32)
            v = v + self.downward.astype(jnp.float32)
        self.upward = lax.ppermute(u.astype(jnp.bfloat16), "col", [(z, z + 1) for z in range(self.n - self.distance)])
        self.downward = lax.ppermute(v.astype(jnp.bfloat16), "col", [(z, z - 1) for z in range(self.distance, self.n)])

    def total(self):
        return self.products[0] + self.upward.astype(jnp.float32) + self.downward.astype(jnp.float32)


def substitute_kernel(rows_n, rhs_ref, head_ref, inverse_ref, solution_ref, solved_ref, current, solved, send_sem, recv_sem, out_sem):
    r = lax.axis_index("row")
    pair = r + 1 - 2 * (r % 2)
    half = rows_n // 2
    tile_rows, width = rhs_ref.shape[1:]
    columns = 256
    own_rows = pl.ds(pl.multiple_of(r * tile_rows, tile_rows), tile_rows)

    barrier = pltpu.get_barrier_semaphore()
    for j in range(1, rows_n):
        pl.semaphore_signal(barrier, inc=1, device_id={"row": (r + j) % rows_n}, device_id_type=pl.DeviceIdType.MESH)
    pl.semaphore_wait(barrier, rows_n - 1)

    sent = []

    def copy(buffer, exchange, owner, slot, device):
        rows = buffer.at[pl.ds(pl.multiple_of(owner * tile_rows, tile_rows), tile_rows)]
        return pltpu.make_async_remote_copy(
            src_ref=rows,
            dst_ref=rows,
            send_sem=send_sem.at[exchange, slot],
            recv_sem=recv_sem.at[exchange, owner],
            device_id={"row": device},
            device_id_type=pl.DeviceIdType.MESH,
        )

    def gather(buffer, exchange):
        for j in range(half - 1, 0, -1):
            sent.append(copy(buffer, exchange, r, j, (r + 2 * j) % rows_n))
            sent[-1].start()
        sent.append(copy(buffer, exchange, r, 0, pair))
        sent[-1].start()
        for j in range(1, half):
            owner = (r + rows_n - 2 * j) % rows_n
            onward = copy(buffer, exchange, owner, half + j, pair)
            onward.wait_recv()
            onward.start()
            sent.append(onward)
        for j in range(half):
            copy(buffer, exchange, (pair + rows_n - 2 * j) % rows_n, 0, pair).wait_recv()

    outward = []
    for k in range(rhs_ref.shape[0]):

        @pl.loop(0, width // columns)
        def _(c):
            cols = pl.ds(pl.multiple_of(c * columns, columns), columns)
            total = rhs_ref[k, :, cols]
            for j in range(k):
                total = total - dot(head_ref[k - 1, j], solved[j, :, cols])
            current[k, own_rows, cols] = total.astype(jnp.bfloat16)

        gather(current.at[k], 2 * k)

        @pl.loop(0, width // columns)
        def _(c):
            cols = pl.ds(pl.multiple_of(c * columns, columns), columns)
            own = dot(inverse_ref[k], current[k, :, cols])
            solution_ref[k, :, cols] = own
            solved[k, own_rows, cols] = own.astype(jnp.bfloat16)

        gather(solved.at[k], 2 * k + 1)
        outward.append(pltpu.make_async_copy(solved.at[k], solved_ref.at[k], out_sem.at[k]))
        outward[-1].start()
    for item in sent:
        item.wait_send()
    for item in outward:
        item.wait()


def substitute(rhs, head, inverse, rows_n):
    steps, tile_rows, width = rhs.shape
    block = rows_n * tile_rows
    vmem = pl.BlockSpec(memory_space=pltpu.VMEM)
    return pl.pallas_call(
        functools.partial(substitute_kernel, rows_n),
        out_shape=(
            jax.ShapeDtypeStruct((steps, tile_rows, width), jnp.float32),
            jax.ShapeDtypeStruct((steps, block, width), jnp.bfloat16),
        ),
        in_specs=[vmem] * 3,
        out_specs=(vmem, pl.BlockSpec(memory_space=pl.ANY)),
        scratch_shapes=[
            pltpu.VMEM((steps, block, width), jnp.bfloat16),
            pltpu.VMEM((steps, block, width), jnp.bfloat16),
            pltpu.SemaphoreType.DMA((2 * steps, rows_n)),
            pltpu.SemaphoreType.DMA((2 * steps, rows_n)),
            pltpu.SemaphoreType.DMA((steps,)),
        ],
        compiler_params=pltpu.CompilerParams(collective_id=0, has_side_effects=True, vmem_limit_bytes=40 * 2**20),
        cost_estimate=pl.CostEstimate(flops=12 * 10**13, bytes_accessed=2**24, transcendentals=0),
    )(rhs, head, inverse)


def shards(rhs, factor, diag_inverse):
    block_count, tile_rows, width = rhs.shape
    panel = factor.shape[3]
    n = lax.axis_size("col")
    rows_n = lax.axis_size("row")
    z = lax.axis_index("col")
    r = lax.axis_index("row")

    head = factor[1:STEPS, :, : STEPS - 1, :].transpose(0, 2, 1, 3)
    head = lax.all_gather(head, "col", axis=3, tiled=True)

    tiles = []
    start = STEPS
    for count in GATHERED:
        flat = factor[start : start + count].reshape(count * tile_rows, STEPS * panel)
        head, flat = lax.optimization_barrier((head, flat))
        tiles.append((start, count, Line(flat, n)))
        start += count

    solution_rows, stacked = substitute(rhs[:STEPS], head, diag_inverse, rows_n)
    for _, _, line in tiles:
        line.hop()
        stacked = line.tie(stacked)

    def panel_of(d):
        return lax.dynamic_slice_in_dim(stacked, ((z + d) % n) * panel, panel, axis=1).reshape(STEPS * panel, width)

    panels = [panel_of(d) for d in range(n)]
    share = panel // rows_n
    pieces = []
    for d in range(1, n):
        target = (z - d) % n
        piece = lax.dynamic_slice_in_dim(stacked, target * panel + r * share, share, axis=1)
        pieces.append(lax.ppermute(piece, "col", [(s, (s - d) % n) for s in range(n)]))
    spread = lax.all_gather(jnp.concatenate(pieces, axis=2), "row", axis=1, tiled=True)
    spread = spread.reshape(STEPS * panel, (n - 1) * width)
    own_panels = [panels[0]] + [spread[:, d * width : (d + 1) * width] for d in range(n - 1)]
    sums = []
    for count in REDUCED:
        flat = factor[start : start + count].reshape(count * tile_rows, STEPS * panel)
        sums.append((start, count, Sums([dot(flat, p) for p in own_panels], n)))
        start += count

    for step in range(1, n):
        if step < n - 1:
            for _, _, line in tiles:
                line.hop()
        for _, _, item in sums:
            item.hop()
        moved = [(line.below[-1], line.above[-1]) for _, _, line in tiles]
        carried = [(item.upward, item.downward) for _, _, item in sums]
        if step < n - 1:
            moved, carried = lax.optimization_barrier((moved, carried))
        for (_, _, line), (below, above) in zip(tiles, moved):
            line.below[-1], line.above[-1] = below, above
        for (_, _, item), (upward, downward) in zip(sums, carried):
            item.upward, item.downward = upward, downward

    outs = []
    for begin, count, line in tiles:
        parts = line.parts()
        total = rhs[begin : begin + count].reshape(count * tile_rows, width)
        for d in range(n):
            total = total - dot(parts[d], panels[d])
        outs.append(total.reshape(count, tile_rows, width))
    for begin, count, item in sums:
        outs.append(rhs[begin : begin + count] - item.total().reshape(count, tile_rows, width))
    return solution_rows, jnp.concatenate(outs)


def solution(mesh):
    in_specs = (P(None, "row", "col"), P(None, "row", None, "col"), P(None, "row", None))
    out_specs = (P(None, "row", "col"), P(None, "row", "col"))
    return jax.shard_map(shards, mesh=mesh, in_specs=in_specs, out_specs=out_specs, check_vma=False)
```
